256 devices in a mesh: rep: 64 (over x_lo, z, y), fsdp: 4 (over x_hi, core).
Axes of the slice: x: 4 (x_hi: 2, x_lo: 2; x = x_hi * 2 + x_lo), y: 4, z: 8, core: 2. Of those that a mesh axis runs over, the one named last changes fastest.
Arguments:
- hidden: bfloat16 [64, 1024, 4096], P('rep', 'fsdp'), may hold values from -6 to 6
- key_grad: bfloat16 [64, 1024, 512], P('rep', 'fsdp'), may hold values from -0.1875 to 0.1875
- weight: float32 [64, 4096, 512], P('rep', 'fsdp'), may hold values from -0.09375 to 0.09375
- moment1: bfloat16 [64, 4096, 512], P('rep', 'fsdp'), may hold values from -3 to 3
- moment2: bfloat16 [64, 4096, 512], P('rep', 'fsdp'), may hold values from 0.19921875 to 2
- step: int32 [], replicated, may hold values from 0 to 999
Outputs:
- keys: bfloat16 [64, 1024, 512], P('rep', 'fsdp')
- input_grad: bfloat16 [64, 1024, 4096], P('rep', 'fsdp')
- weight_next: float32 [64, 4096, 512], P('rep', 'fsdp')
- moment1_next: bfloat16 [64, 4096, 512], P('rep', 'fsdp')
- moment2_next: bfloat16 [64, 4096, 512], P('rep', 'fsdp')
The draws below stay inside these ranges and needn't reach their ends.
All inputs are finite; a program needn't handle non-finite values.
Results may differ from the reference program's by a relative error of at most 0.005.
Values may be sent and summed in bfloat16 or wider, within the bound.
A program may use at most 64 MiB of HBM per device.

```python
import math
import jax
import jax.numpy as jnp
from jax import lax

D = 4096
KV = 512
TOK_REP = 1024
LEVELS = 6
N_REP = 64


def with_spikes(drawn, rng, source, target, parts, factor):
    owner, partner = [(jnp.arange(drawn.shape[axis_at]) // (drawn.shape[axis_at] // parts)).reshape([-1 if axis == axis_at else 1 for axis in range(drawn.ndim)]) for axis_at in (source, target)]
    chosen = jax.random.permutation(rng, parts)[partner]
    strong = (owner == chosen) | (owner == (partner + parts // 2) % parts)
    return jnp.where(strong, factor * drawn, drawn)


def level_of(rng, extent, pieces, smallest, top_value):
    loudness, own = 1.0, jax.random.fold_in(rng, 6)
    for axis_at, parts in pieces:
        heights = jnp.exp(jax.random.uniform(jax.random.fold_in(own, axis_at), (parts,), jnp.float32, smallest / len(pieces), top_value / len(pieces)))
        loudness = loudness * jnp.repeat(heights, extent[axis_at] // parts).reshape([-1 if axis == axis_at else 1 for axis in range(len(extent))])
    return loudness


def noise(rng, shape, spread, reach, shards=(), dtype=jnp.bfloat16):
    values = spread * jax.random.normal(rng, shape, jnp.float32)
    if shards:
        values = values * level_of(rng, shape, shards, -0.22, 0.18)
    return jnp.clip(values, -reach, reach).astype(dtype)


def gaussian_with(own_key, dims, deviation, bound, pieces, heavy, held_as=jnp.bfloat16):
    entries = deviation * jax.random.normal(own_key, dims, jnp.float32)
    if pieces:
        entries = entries * level_of(own_key, dims, pieces, -0.22, 0.18)
    return jnp.clip(with_spikes(entries, jax.random.fold_in(own_key, 3), *heavy), -bound, bound).astype(held_as)


def setup_inputs(seed: int = 0) -> dict:
    streams_of = jax.random.split(jax.random.key(seed), 7)
    return {
        "hidden": gaussian_with(streams_of[0], (N_REP, TOK_REP, D), 1.0, 6.0, ((0, 64), (1, 4)), (1, 2, 4, 2.0)),
        "key_grad": noise(streams_of[1], (N_REP, TOK_REP, KV), TOK_REP ** -0.5, 0.1875, ((0, 64), (1, 4))),
        "weight": noise(streams_of[2], (N_REP, D, KV), D ** -0.5, 0.09375, ((0, 64), (1, 4)), jnp.float32),
        "moment1": noise(streams_of[3], (N_REP, D, KV), 0.3, 3.0, ((0, 64), (1, 4))),
        "moment2": jnp.clip(jnp.exp(math.log(2.0) - 2.306499 * jax.random.uniform(streams_of[4], (N_REP, D, KV), jnp.float32) ** level_of(streams_of[4], (N_REP, D, KV), ((0, 64), (1, 4)), -0.2, 0.2)), 0.19921875, 2.0).astype(jnp.bfloat16),
        "step": jax.random.randint(streams_of[5], (), 0, 1000).astype(jnp.int32),
    }


def replica_pass(operands):
    tokens_in, cotangent, weight_half = operands
    keys_full = jnp.dot(tokens_in, weight_half, preferred_element_type=jnp.float32)
    back_full = lax.dot_general(cotangent, weight_half, (((1,), (1,)), ((), ())), preferred_element_type=jnp.float32)
    grad_full = lax.dot_general(tokens_in, cotangent, (((0,), (0,)), ((), ())), preferred_element_type=jnp.float32)
    return (keys_full.astype(jnp.bfloat16), back_full.astype(jnp.bfloat16), grad_full)

def reference(hidden, key_grad, weight, moment1, moment2, step):
    weight_half = weight.astype(jnp.bfloat16)
    keys, input_grad, grad = lax.map(replica_pass, (hidden, key_grad, weight_half))
    count = (step + 1).astype(jnp.float32)
    first = 0.9 * moment1.astype(jnp.float32) + 0.1 * grad
    second = 0.95 * moment2.astype(jnp.float32) + 0.05 * grad * grad
    first_hat = first / (1.0 - jnp.power(jnp.float32(0.9), count))
    second_hat = second / (1.0 - jnp.power(jnp.float32(0.95), count))
    updated = weight - 0.003 * (first_hat / (jnp.sqrt(second_hat) + 1e-08) + 0.1 * weight)
    distance = jnp.left_shift(jnp.int32(1), (step % LEVELS).astype(jnp.int32)) % N_REP
    neighbour = jnp.roll(updated, distance, axis=0)
    weight_next = 0.5 * (updated + neighbour)
    return (keys, input_grad, weight_next, first.astype(jnp.bfloat16), second.astype(jnp.bfloat16))
```

```python
import functools
import math

import jax
import jax.numpy as jnp
from jax import lax
from jax.experimental import pallas as pl
from jax.experimental.pallas import tpu as pltpu
from jax.sharding import PartitionSpec as P

LEVELS = 6
MESH = pl.DeviceIdType.MESH
F32 = jnp.float32
BF16 = jnp.bfloat16
CHUNKS = 8
TOKENS_MAJOR = (((0,), (0,)), ((), ()))
FEATURES_MINOR = (((1,), (1,)), ((), ()))


def train_kernel(
    distance,
    step_ref,
    hidden_ref,
    cot_ref,
    weight_ref,
    mom1_ref,
    mom2_ref,
    keys_ref,
    dx_ref,
    wnext_ref,
    mom1_out,
    mom2_out,
    x_own,
    x_pair,
    dy_own,
    dy_pair,
    wbuf,
    m1buf,
    m2buf,
    wfull,
    part_out,
    part_in,
    ubuf,
    nbuf,
    dxbuf,
    kacc,
    kbuf,
    load_sem,
    xs_sem,
    xr_sem,
    own_sem,
    ags_sem,
    agr_sem,
    fws_sem,
    fwr_sem,
    ps_sem,
    pr_sem,
    gs_sem,
    gr_sem,
    m1o_sem,
    m2o_sem,
    wo_sem,
    dxo_sem,
    ko_sem,
):
    rep, shard = lax.axis_index("rep"), lax.axis_index("fsdp")
    replicas = lax.axis_size("rep")
    rows = weight_ref.shape[0]
    chunk = rows // CHUNKS
    core = lax.rem(shard, 2)
    half = shard // 2
    pair_shard = half * 2 + (1 - core)
    far_shard = (1 - half) * 2 + core
    diag_shard = (1 - half) * 2 + (1 - core)
    pair, far = (rep, pair_shard), (rep, far_shard)
    target = (lax.rem(rep + distance, replicas), shard)
    source = (lax.rem(rep - distance + replicas, replicas), shard)

    def at(which, k, size=chunk):
        return pl.ds(pl.multiple_of(which * rows + k * chunk, chunk), size)

    def remote(src, dst, send, recv, device):
        return pltpu.make_async_remote_copy(
            src_ref=src, dst_ref=dst, send_sem=send, recv_sem=recv, device_id=device, device_id_type=MESH
        )

    loads = [
        pltpu.make_async_copy(weight_ref, wbuf, load_sem.at[0]),
        pltpu.make_async_copy(cot_ref, dy_own, load_sem.at[1]),
        pltpu.make_async_copy(hidden_ref, x_own, load_sem.at[2]),
        pltpu.make_async_copy(mom1_ref, m1buf, load_sem.at[3]),
        pltpu.make_async_copy(mom2_ref, m2buf, load_sem.at[4]),
    ]
    for load in loads:
        load.start()

    barrier = pltpu.get_barrier_semaphore()
    for peer in (pair, far, target, source):
        pl.semaphore_signal(barrier, inc=1, device_id=peer, device_id_type=MESH)
    pl.semaphore_wait(barrier, 4)

    give = [
        remote(cot_ref, dy_pair, xs_sem.at[0], xr_sem.at[0], pair),
        remote(hidden_ref.at[:, at(diag_shard, 0, rows)], x_pair.at[0], xs_sem.at[1], xr_sem.at[1], pair),
        remote(hidden_ref.at[:, at(pair_shard, 0, rows)], x_pair.at[1], xs_sem.at[2], xr_sem.at[2], pair),
    ]
    for copy in give:
        copy.start()

    loads[0].wait()

    def cast(k, carry):
        part = pl.ds(pl.multiple_of(k * chunk, chunk), chunk)
        wfull[at(shard, k), :] = wbuf[part, :].astype(BF16)
        return carry

    lax.fori_loop(0, CHUNKS, cast, 0)

    def gather(k):
        return remote(wfull.at[at(shard, k)], wfull.at[at(shard, k)], ags_sem.at[k], agr_sem.at[k], far)

    def forward(k):
        return remote(wfull.at[at(far_shard, k)], wfull.at[at(far_shard, k)], fws_sem.at[k], fwr_sem.at[k], pair)

    own_block = remote(
        wfull.at[at(shard, 0, rows)], wfull.at[at(shard, 0, rows)], own_sem.at[0], own_sem.at[1], pair
    )

    def partial_copy(k):
        return remote(part_out.at[k], part_in.at[k], ps_sem.at[k], pr_sem.at[k], far)

    def gossip(k):
        return remote(ubuf.at[k], nbuf.at[k], gs_sem.at[k], gr_sem.at[k], target)

    loads[1].wait()
    loads[2].wait()
    gather(0).start()
    own_block.start()
    give[0].wait_recv()
    give[1].wait_recv()

    def grad_chunk(which, slot, k):
        columns = pl.ds(pl.multiple_of(k * chunk, chunk), chunk)
        mine = lax.dot_general(
            x_own[:, at(which, k)], dy_own[...], TOKENS_MAJOR, preferred_element_type=F32
        )
        return mine + lax.dot_general(
            x_pair[slot, :, columns], dy_pair[...], TOKENS_MAJOR, preferred_element_type=F32
        )

    def partials(k, carry):
        part_out[k] = grad_chunk(far_shard, 0, k).astype(BF16)

        @pl.when(k > 0)
        def _():
            partial_copy(k - 1).start()

        return carry

    lax.fori_loop(0, CHUNKS, partials, 0)
    kacc[...] = jnp.zeros_like(kacc)
    partial_copy(CHUNKS - 1).start()

    def dx_store(which, k):
        return pltpu.make_async_copy(
            dxbuf.at[:, at(which, k)], dx_ref.at[:, at(which, k)], dxo_sem.at[which, k]
        )

    def project(which, k):
        block = wfull[at(which, k), :]
        kacc[...] += jnp.dot(x_own[:, at(which, k)], block, preferred_element_type=F32)
        dxbuf[:, at(which, k)] = lax.dot_general(
            dy_own[...], block, FEATURES_MINOR, preferred_element_type=F32
        ).astype(BF16)

    def part_of(k):
        return pl.ds(pl.multiple_of(k * chunk, chunk), chunk)

    def m1_store(k):
        return pltpu.make_async_copy(m1buf.at[part_of(k)], mom1_out.at[part_of(k)], m1o_sem.at[k])

    def m2_store(k):
        return pltpu.make_async_copy(m2buf.at[part_of(k)], mom2_out.at[part_of(k)], m2o_sem.at[k])

    def w_store(k):
        return pltpu.make_async_copy(wbuf.at[part_of(k)], wnext_ref.at[part_of(k)], wo_sem.at[k])

    loads[3].wait()
    loads[4].wait()
    give[2].wait_recv()
    own_block.wait_recv()
    count = jnp.full((8, 128), step_ref[0] + 1, jnp.int32).astype(F32)
    scale1 = (1.0 / (1.0 - jnp.exp(count * math.log(0.9))))[:1, :1]
    scale2 = (1.0 / (1.0 - jnp.exp(count * math.log(0.95))))[:1, :1]

    def update(k, carry):
        mine = grad_chunk(shard, 1, k)

        @pl.when(k < CHUNKS - 1)
        def _():
            gather(k + 1).start()

        partial_copy(k).wait_recv()
        grad = mine + part_in[k].astype(F32)
        part = part_of(k)
        first = 0.9 * m1buf[part, :].astype(F32) + 0.1 * grad
        second = 0.95 * m2buf[part, :].astype(F32) + 0.05 * grad * grad
        m1buf[part, :] = first.astype(BF16)
        m2buf[part, :] = second.astype(BF16)
        weight = wbuf[part, :]
        new = weight - 0.003 * ((first * scale1) / (jnp.sqrt(second * scale2) + 1e-08) + 0.1 * weight)
        wbuf[part, :] = new
        ubuf[k] = new.astype(BF16)
        m1_store(k).start()
        m2_store(k).start()
        project(shard, k)
        gossip(k).start()
        project(pair_shard, k)
        dx_store(shard, k).start()
        dx_store(pair_shard, k).start()
        return carry

    lax.fori_loop(0, CHUNKS, update, 0)

    def finish(k, carry):
        gather(k).wait_recv()
        forward(k).start()
        project(far_shard, k)
        dx_store(far_shard, k).start()
        forward(k).wait_recv()
        project(diag_shard, k)
        dx_store(diag_shard, k).start()

        @pl.when(k == CHUNKS - 1)
        def _():
            kbuf[...] = kacc[...].astype(BF16)
            pltpu.make_async_copy(kbuf, keys_ref, ko_sem).start()

        gossip(k).wait_recv()
        part = part_of(k)
        wbuf[part, :] = 0.5 * (wbuf[part, :] + nbuf[k].astype(F32))
        w_store(k).start()
        return carry

    lax.fori_loop(0, CHUNKS, finish, 0)

    for copy in give:
        copy.wait_send()
    own_block.wait_send()

    def drain(k, carry):
        gather(k).wait_send()
        forward(k).wait_send()
        partial_copy(k).wait_send()
        gossip(k).wait_send()
        m1_store(k).wait()
        m2_store(k).wait()
        for which in (shard, pair_shard, far_shard, diag_shard):
            dx_store(which, k).wait()
        w_store(k).wait()
        return carry

    lax.fori_loop(0, CHUNKS, drain, 0)
    pltpu.make_async_copy(kbuf, keys_ref, ko_sem).wait()


def make_train(level, replicas):
    distance = 2**level % replicas

    def train(step, hidden, cotangent, weight, moment1, moment2):
        (tokens, width), (rows, features) = hidden.shape, weight.shape
        chunk = rows // CHUNKS
        dma = pltpu.SemaphoreType.DMA
        per_chunk = dma((CHUNKS,))
        hbm = pl.BlockSpec(memory_space=pl.ANY)
        return pl.pallas_call(
            functools.partial(train_kernel, distance),
            name=f"train_{distance}",
            out_shape=(
                jax.ShapeDtypeStruct((tokens, features), BF16),
                jax.ShapeDtypeStruct((tokens, width), BF16),
                jax.ShapeDtypeStruct((rows, features), F32),
                jax.ShapeDtypeStruct((rows, features), BF16),
                jax.ShapeDtypeStruct((rows, features), BF16),
            ),
            in_specs=[pl.BlockSpec(memory_space=pltpu.SMEM)] + [hbm] * 5,
            out_specs=(hbm,) * 5,
            scratch_shapes=[
                pltpu.VMEM((tokens, width), BF16),
                pltpu.VMEM((2, tokens, rows), BF16),
                pltpu.VMEM((tokens, features), BF16),
                pltpu.VMEM((tokens, features), BF16),
                pltpu.VMEM((rows, features), F32),
                pltpu.VMEM((rows, features), BF16),
                pltpu.VMEM((rows, features), BF16),
                pltpu.VMEM((width, features), BF16),
                pltpu.VMEM((CHUNKS, chunk, features), BF16),
                pltpu.VMEM((CHUNKS, chunk, features), BF16),
                pltpu.VMEM((CHUNKS, chunk, features), BF16),
                pltpu.VMEM((CHUNKS, chunk, features), BF16),
                pltpu.VMEM((tokens, width), BF16),
                pltpu.VMEM((tokens, features), F32),
                pltpu.VMEM((tokens, features), BF16),
                dma((5,)),
                dma((3,)),
                dma((3,)),
                dma((2,)),
                per_chunk,
                per_chunk,
                per_chunk,
                per_chunk,
                per_chunk,
                per_chunk,
                per_chunk,
                per_chunk,
                per_chunk,
                per_chunk,
                per_chunk,
                dma((4, CHUNKS)),
                dma,
            ],
            compiler_params=pltpu.CompilerParams(
                collective_id=level, has_side_effects=True, vmem_limit_bytes=56 << 20
            ),
        )(step, hidden, cotangent, weight, moment1, moment2)

    return train


def per_device(hidden, key_grad, weight, moment1, moment2, step):
    branches = [make_train(level, lax.axis_size("rep")) for level in range(LEVELS)]
    outs = lax.switch(
        step % LEVELS,
        branches,
        step.reshape(1),
        hidden[0],
        key_grad[0],
        weight[0],
        moment1[0],
        moment2[0],
    )
    return tuple(out[None] for out in outs)


def solution(mesh):
    blocks = P("rep", "fsdp", None)
    return jax.shard_map(
        per_device,
        mesh=mesh,
        in_specs=(blocks,) * 5 + (P(),),
        out_specs=(blocks,) * 5,
        check_vma=False,
    )
```

```python
import functools
import math

import jax
import jax.numpy as jnp
from jax import lax
from jax.experimental import pallas as pl
from jax.experimental.pallas import tpu as pltpu
from jax.sharding import PartitionSpec as P

LEVELS = 6
MESH = pl.DeviceIdType.MESH
F32 = jnp.float32
BF16 = jnp.bfloat16
CHUNKS = 8
ROUTES = ((0, -4, 5, 1), (0, -4, 6, 2), (0, -4, 8, 4), (0, 8), (0, 16), (32,))
TOKENS_MAJOR = (((0,), (0,)), ((), ()))
FEATURES_MINOR = (((1,), (1,)), ((), ()))


def train_kernel(
    distance,
    routes,
    step_ref,
    hidden_ref,
    cot_ref,
    weight_ref,
    mom1_ref,
    mom2_ref,
    keys_ref,
    dx_ref,
    wnext_ref,
    mom1_out,
    mom2_out,
    x_own,
    x_pair,
    dy_own,
    dy_pair,
    wbuf,
    m1buf,
    m2buf,
    wfull,
    part_out,
    part_in,
    ubuf,
    nbuf,
    rbuf,
    dxbuf,
    kacc,
    kbuf,
    load_sem,
    xs_sem,
    xr_sem,
    own_sem,
    ags_sem,
    agr_sem,
    fws_sem,
    fwr_sem,
    ps_sem,
    pr_sem,
    gs_sem,
    gr_sem,
    rr_sem,
    rf_sem,
    m1o_sem,
    m2o_sem,
    wo_sem,
    dxo_sem,
    ko_sem,
):
    rep, shard = lax.axis_index("rep"), lax.axis_index("fsdp")
    replicas = lax.axis_size("rep")
    rows = weight_ref.shape[0]
    chunk = rows // CHUNKS
    core = lax.rem(shard, 2)
    half = shard // 2
    pair_shard = half * 2 + (1 - core)
    far_shard = (1 - half) * 2 + core
    diag_shard = (1 - half) * 2 + (1 - core)
    pair, far = (rep, pair_shard), (rep, far_shard)
    target = (lax.rem(rep + distance, replicas), shard)
    source = (lax.rem(rep - distance + replicas, replicas), shard)
    block = replicas // 2
    side, row = rep // block, lax.rem(rep, block)

    def device(other, r):
        return (1 - side if other else side) * block + lax.rem(r + 2 * block, block), shard

    crossing = row + distance >= block
    relayed = [r for r in routes if r != distance]
    peers = [pair, far, target, source]
    for r in relayed:
        peers += [device(True, row + r), device(True, row - r)]
        peers += [device(False, row - r + distance), device(False, row + r - distance)]

    def at(which, k, size=chunk):
        return pl.ds(pl.multiple_of(which * rows + k * chunk, chunk), size)

    def remote(src, dst, send, recv, device):
        return pltpu.make_async_remote_copy(
            src_ref=src, dst_ref=dst, send_sem=send, recv_sem=recv, device_id=device, device_id_type=MESH
        )

    loads = [
        pltpu.make_async_copy(weight_ref, wbuf, load_sem.at[0]),
        pltpu.make_async_copy(cot_ref, dy_own, load_sem.at[1]),
        pltpu.make_async_copy(hidden_ref, x_own, load_sem.at[2]),
        pltpu.make_async_copy(mom1_ref, m1buf, load_sem.at[3]),
        pltpu.make_async_copy(mom2_ref, m2buf, load_sem.at[4]),
    ]
    for load in loads:
        load.start()

    barrier = pltpu.get_barrier_semaphore()
    for peer in peers:
        pl.semaphore_signal(barrier, inc=1, device_id=peer, device_id_type=MESH)
    pl.semaphore_wait(barrier, len(peers))

    give = [
        remote(cot_ref, dy_pair, xs_sem.at[0], xr_sem.at[0], pair),
        remote(hidden_ref.at[:, at(diag_shard, 0, rows)], x_pair.at[0], xs_sem.at[1], xr_sem.at[1], pair),
        remote(hidden_ref.at[:, at(pair_shard, 0, rows)], x_pair.at[1], xs_sem.at[2], xr_sem.at[2], pair),
    ]
    for copy in give:
        copy.start()

    loads[0].wait()

    def cast(k, carry):
        part = pl.ds(pl.multiple_of(k * chunk, chunk), chunk)
        wfull[at(shard, k), :] = wbuf[part, :].astype(BF16)
        return carry

    lax.fori_loop(0, CHUNKS, cast, 0)

    def gather(k):
        return remote(wfull.at[at(shard, k)], wfull.at[at(shard, k)], ags_sem.at[k], agr_sem.at[k], far)

    def forward(k):
        return remote(wfull.at[at(far_shard, k)], wfull.at[at(far_shard, k)], fws_sem.at[k], fwr_sem.at[k], pair)

    own_block = remote(
        wfull.at[at(shard, 0, rows)], wfull.at[at(shard, 0, rows)], own_sem.at[0], own_sem.at[1], pair
    )

    def partial_copy(k):
        return remote(part_out.at[k], part_in.at[k], ps_sem.at[k], pr_sem.at[k], far)

    def gossip(k):
        return remote(ubuf.at[k], nbuf.at[k], gs_sem.at[k], gr_sem.at[k], target)

    def to_relay(k, r):
        return remote(ubuf.at[k], rbuf.at[k], gs_sem.at[k], rr_sem.at[k], device(True, row + r))

    def from_relay(k, r):
        return remote(rbuf.at[k], nbuf.at[k], rf_sem.at[k], gr_sem.at[k], device(False, row - r + distance))

    def send_gossip(k):
        for i, r in enumerate(routes):
            mine = lax.rem(k, len(routes)) == i
            if r == distance:
                pl.when(mine)(lambda: gossip(k).start())
            else:
                pl.when(mine & crossing)(lambda: to_relay(k, r).start())
                pl.when(mine & jnp.logical_not(crossing))(lambda: gossip(k).start())

    def relaying(k, act):
        for i, r in enumerate(routes):
            if r != distance:
                origin = lax.rem(row - r + 2 * block, block)
                pl.when((lax.rem(k, len(routes)) == i) & (origin + distance >= block))(lambda: act(k, r))

    def pass_on(k, r):
        to_relay(k, r).wait_recv()
        from_relay(k, r).start()

    loads[1].wait()
    loads[2].wait()
    gather(0).start()
    own_block.start()
    give[0].wait_recv()
    give[1].wait_recv()

    def grad_chunk(which, slot, k):
        columns = pl.ds(pl.multiple_of(k * chunk, chunk), chunk)
        mine = lax.dot_general(
            x_own[:, at(which, k)], dy_own[...], TOKENS_MAJOR, preferred_element_type=F32
        )
        return mine + lax.dot_general(
            x_pair[slot, :, columns], dy_pair[...], TOKENS_MAJOR, preferred_element_type=F32
        )

    def partials(k, carry):
        part_out[k] = grad_chunk(far_shard, 0, k).astype(BF16)

        @pl.when(k > 0)
        def _():
            partial_copy(k - 1).start()

        return carry

    lax.fori_loop(0, CHUNKS, partials, 0)
    kacc[...] = jnp.zeros_like(kacc)
    partial_copy(CHUNKS - 1).start()

    def dx_store(which, k):
        return pltpu.make_async_copy(
            dxbuf.at[:, at(which, k)], dx_ref.at[:, at(which, k)], dxo_sem.at[which, k]
        )

    def project(which, k):
        block = wfull[at(which, k), :]
        kacc[...] += jnp.dot(x_own[:, at(which, k)], block, preferred_element_type=F32)
        dxbuf[:, at(which, k)] = lax.dot_general(
            dy_own[...], block, FEATURES_MINOR, preferred_element_type=F32
        ).astype(BF16)

    def part_of(k):
        return pl.ds(pl.multiple_of(k * chunk, chunk), chunk)

    def m1_store(k):
        return pltpu.make_async_copy(m1buf.at[part_of(k)], mom1_out.at[part_of(k)], m1o_sem.at[k])

    def m2_store(k):
        return pltpu.make_async_copy(m2buf.at[part_of(k)], mom2_out.at[part_of(k)], m2o_sem.at[k])

    def w_store(k):
        return pltpu.make_async_copy(wbuf.at[part_of(k)], wnext_ref.at[part_of(k)], wo_sem.at[k])

    loads[3].wait()
    loads[4].wait()
    give[2].wait_recv()
    own_block.wait_recv()
    count = jnp.full((8, 128), step_ref[0] + 1, jnp.int32).astype(F32)
    scale1 = (1.0 / (1.0 - jnp.exp(count * math.log(0.9))))[:1, :1]
    scale2 = (1.0 / (1.0 - jnp.exp(count * math.log(0.95))))[:1, :1]

    def start_gather(k, carry):
        gather(k).start()
        return carry

    def update(k, carry):
        mine = grad_chunk(shard, 1, k)
        if not relayed:
            pl.when(k < CHUNKS - 1)(lambda: gather(k + 1).start())

        partial_copy(k).wait_recv()
        grad = mine + part_in[k].astype(F32)
        part = part_of(k)
        first = 0.9 * m1buf[part, :].astype(F32) + 0.1 * grad
        second = 0.95 * m2buf[part, :].astype(F32) + 0.05 * grad * grad
        m1buf[part, :] = first.astype(BF16)
        m2buf[part, :] = second.astype(BF16)
        weight = wbuf[part, :]
        new = weight - 0.003 * ((first * scale1) / (jnp.sqrt(second * scale2) + 1e-08) + 0.1 * weight)
        wbuf[part, :] = new
        ubuf[k] = new.astype(BF16)
        m1_store(k).start()
        m2_store(k).start()
        project(shard, k)
        send_gossip(k)

        if relayed:
            @pl.when(k == CHUNKS - 2)
            def _():
                lax.fori_loop(1, 3, start_gather, 0)

            @pl.when(k == CHUNKS - 1)
            def _():
                lax.fori_loop(3, CHUNKS, start_gather, 0)

        project(pair_shard, k)
        dx_store(shard, k).start()
        dx_store(pair_shard, k).start()
        return carry

    lax.fori_loop(0, CHUNKS, update, 0)

    def finish(k, carry):
        @pl.when((k > 0) & (2 * k <= CHUNKS))
        def _():
            relaying(2 * k - 2, pass_on)
            relaying(2 * k - 1, pass_on)

        gather(k).wait_recv()
        forward(k).start()
        project(far_shard, k)
        dx_store(far_shard, k).start()
        forward(k).wait_recv()
        project(diag_shard, k)
        dx_store(diag_shard, k).start()

        @pl.when(k > 1)
        def _():
            settle(k - 2)

        return carry

    def settle(k):
        gossip(k).wait_recv()
        part = part_of(k)
        wbuf[part, :] = 0.5 * (wbuf[part, :] + nbuf[k].astype(F32))
        w_store(k).start()

    lax.fori_loop(0, CHUNKS, finish, 0)
    kbuf[...] = kacc[...].astype(BF16)
    pltpu.make_async_copy(kbuf, keys_ref, ko_sem).start()

    def settle_rest(k, carry):
        settle(k)
        return carry

    lax.fori_loop(CHUNKS - 2, CHUNKS, settle_rest, 0)

    for copy in give:
        copy.wait_send()
    own_block.wait_send()

    def drain(k, carry):
        gather(k).wait_send()
        forward(k).wait_send()
        partial_copy(k).wait_send()
        gossip(k).wait_send()
        relaying(k, lambda k, r: from_relay(k, r).wait_send())
        m1_store(k).wait()
        m2_store(k).wait()
        for which in (shard, pair_shard, far_shard, diag_shard):
            dx_store(which, k).wait()
        w_store(k).wait()
        return carry

    lax.fori_loop(0, CHUNKS, drain, 0)
    pltpu.make_async_copy(kbuf, keys_ref, ko_sem).wait()


def make_train(level, replicas):
    distance = 2**level % replicas
    routes = ROUTES[level]

    def train(step, hidden, cotangent, weight, moment1, moment2):
        (tokens, width), (rows, features) = hidden.shape, weight.shape
        chunk = rows // CHUNKS
        dma = pltpu.SemaphoreType.DMA
        per_chunk = dma((CHUNKS,))
        hbm = pl.BlockSpec(memory_space=pl.ANY)
        outs = pl.pallas_call(
            functools.partial(train_kernel, distance, routes),
            name=f"train_{distance}",
            out_shape=(
                jax.ShapeDtypeStruct((tokens, features), BF16),
                jax.ShapeDtypeStruct((tokens, width), BF16),
                jax.ShapeDtypeStruct((rows, features), F32),
                jax.ShapeDtypeStruct((rows, features), BF16),
                jax.ShapeDtypeStruct((rows, features), BF16),
            ),
            in_specs=[pl.BlockSpec(memory_space=pltpu.SMEM)] + [hbm] * 5,
            out_specs=(hbm,) * 5,
            scratch_shapes=[
                pltpu.VMEM((tokens, width), BF16),
                pltpu.VMEM((2, tokens, rows), BF16),
                pltpu.VMEM((tokens, features), BF16),
                pltpu.VMEM((tokens, features), BF16),
                pltpu.VMEM((rows, features), F32),
                pltpu.VMEM((rows, features), BF16),
                pltpu.VMEM((rows, features), BF16),
                pltpu.VMEM((width, features), BF16),
                pltpu.VMEM((CHUNKS, chunk, features), BF16),
                pltpu.VMEM((CHUNKS, chunk, features), BF16),
                pltpu.VMEM((CHUNKS, chunk, features), BF16),
                pltpu.VMEM((CHUNKS, chunk, features), BF16),
                pltpu.VMEM((CHUNKS, chunk, features), BF16),
                pltpu.VMEM((tokens, width), BF16),
                pltpu.VMEM((tokens, features), F32),
                pltpu.VMEM((tokens, features), BF16),
                dma((5,)),
                dma((3,)),
                dma((3,)),
                dma((2,)),
                per_chunk,
                per_chunk,
                per_chunk,
                per_chunk,
                per_chunk,
                per_chunk,
                per_chunk,
                per_chunk,
                per_chunk,
                per_chunk,
                per_chunk,
                per_chunk,
                per_chunk,
                dma((4, CHUNKS)),
                dma,
            ],
            compiler_params=pltpu.CompilerParams(
                collective_id=level, has_side_effects=True, vmem_limit_bytes=32 << 20
            ),
        )(step, hidden, cotangent, weight, moment1, moment2)
        return placed(outs)

    return train


PIECES = (1, 4, 4, 2, 2)


def placed_kernel(*refs):
    half = len(refs) // 2
    ins, outs, sem = refs[:half], refs[half:-1], refs[-1]
    copies = []
    for src, dst, pieces in zip(ins, outs, PIECES):
        size = src.shape[0] // pieces
        for i in range(pieces):
            part = pl.ds(i * size, size)
            copies.append(pltpu.make_async_copy(src.at[part], dst.at[part], sem.at[len(copies)]))
            copies[-1].start()
    for copy in copies:
        copy.wait()


def placed(values):
    hbm = pl.BlockSpec(memory_space=pl.ANY)
    return pl.pallas_call(
        placed_kernel,
        name="placed",
        out_shape=tuple(jax.ShapeDtypeStruct(v.shape, v.dtype) for v in values),
        in_specs=[hbm] * len(values),
        out_specs=(hbm,) * len(values),
        scratch_shapes=[pltpu.SemaphoreType.DMA((sum(PIECES),))],
        compiler_params=pltpu.CompilerParams(vmem_limit_bytes=1 << 20),
    )(*values)


def per_device(hidden, key_grad, weight, moment1, moment2, step):
    branches = [make_train(level, lax.axis_size("rep")) for level in range(LEVELS)]
    outs = lax.switch(
        step % LEVELS,
        branches,
        step.reshape(1),
        hidden[0],
        key_grad[0],
        weight[0],
        moment1[0],
        moment2[0],
    )
    return tuple(out[None] for out in outs)


def solution(mesh):
    blocks = P("rep", "fsdp", None)
    return jax.shard_map(
        per_device,
        mesh=mesh,
        in_specs=(blocks,) * 5 + (P(),),
        out_specs=(blocks,) * 5,
        check_vma=False,
    )
```

```python
import functools
import math

import jax
import jax.numpy as jnp
from jax import lax
from jax.experimental import pallas as pl
from jax.experimental.pallas import tpu as pltpu
from jax.sharding import PartitionSpec as P

LEVELS = 6
MESH = pl.DeviceIdType.MESH
F32 = jnp.float32
BF16 = jnp.bfloat16
CHUNKS = 8
NEAR = (-12, -16, -8, -4, -12, 0, 0)
ROUTES = ((1, *NEAR), (2, *NEAR), (4, *NEAR), (8, -12, 8, -12, -12, 0, 0, 0), (16, 16, 16, 0, 0, 0, 0, 0), (32,) * CHUNKS)
RELAY_LAG = 3
TOKENS_MAJOR = (((0,), (0,)), ((), ()))
FEATURES_MINOR = (((1,), (1,)), ((), ()))


def train_kernel(
    distance,
    routes,
    step_ref,
    hidden_ref,
    cot_ref,
    weight_ref,
    mom1_ref,
    mom2_ref,
    keys_ref,
    dx_ref,
    wnext_ref,
    mom1_out,
    mom2_out,
    x_own,
    x_pair,
    dy_own,
    dy_pair,
    wbuf,
    m1buf,
    m2buf,
    wfull,
    part_out,
    part_in,
    ubuf,
    nbuf,
    rbuf,
    kacc,
    load_sem,
    xs_sem,
    xr_sem,
    own_sem,
    ags_sem,
    agr_sem,
    fws_sem,
    fwr_sem,
    ps_sem,
    pr_sem,
    gs_sem,
    gr_sem,
    rr_sem,
    rf_sem,
):
    rep, shard = lax.axis_index("rep"), lax.axis_index("fsdp")
    replicas = lax.axis_size("rep")
    rows = weight_ref.shape[0]
    chunk = rows // CHUNKS
    core = lax.rem(shard, 2)
    half = shard // 2
    pair_shard = half * 2 + (1 - core)
    far_shard = (1 - half) * 2 + core
    diag_shard = (1 - half) * 2 + (1 - core)
    pair, far = (rep, pair_shard), (rep, far_shard)
    target = (lax.rem(rep + distance, replicas), shard)
    source = (lax.rem(rep - distance + replicas, replicas), shard)
    block = replicas // 2
    side, row = rep // block, lax.rem(rep, block)

    def device(other, r):
        return (1 - side if other else side) * block + lax.rem(r + 2 * block, block), shard

    crossing = row + distance >= block
    relayed = sorted(set(routes) - {distance})
    peers = [pair, far, target, source]
    for r in relayed:
        peers += [device(True, row + r), device(True, row - r)]
        peers += [device(False, row - r + distance), device(False, row + r - distance)]

    def at(which, k, size=chunk):
        return pl.ds(pl.multiple_of(which * rows + k * chunk, chunk), size)

    def remote(src, dst, send, recv, device):
        return pltpu.make_async_remote_copy(
            src_ref=src, dst_ref=dst, send_sem=send, recv_sem=recv, device_id=device, device_id_type=MESH
        )

    loads = [
        pltpu.make_async_copy(weight_ref, wbuf, load_sem.at[0]),
        pltpu.make_async_copy(cot_ref, dy_own, load_sem.at[1]),
        pltpu.make_async_copy(hidden_ref, x_own, load_sem.at[2]),
        pltpu.make_async_copy(mom1_ref, m1buf, load_sem.at[3]),
        pltpu.make_async_copy(mom2_ref, m2buf, load_sem.at[4]),
    ]
    for load in loads:
        load.start()

    barrier = pltpu.get_barrier_semaphore()
    for peer in peers:
        pl.semaphore_signal(barrier, inc=1, device_id=peer, device_id_type=MESH)
    loads[0].wait()

    def cast(k, carry):
        part = pl.ds(pl.multiple_of(k * chunk, chunk), chunk)
        wfull[at(shard, k), :] = wbuf[part, :].astype(BF16)
        return carry

    lax.fori_loop(0, CHUNKS, cast, 0)

    loads[1].wait()
    loads[2].wait()
    pl.semaphore_wait(barrier, len(peers))

    give = [
        remote(cot_ref, dy_pair, xs_sem.at[0], xr_sem.at[0], pair),
        remote(hidden_ref.at[:, at(diag_shard, 0, rows)], x_pair.at[0], xs_sem.at[1], xr_sem.at[1], pair),
        remote(hidden_ref.at[:, at(pair_shard, 0, rows)], x_pair.at[1], xs_sem.at[2], xr_sem.at[2], pair),
    ]
    for copy in give:
        copy.start()

    def gather(k):
        return remote(wfull.at[at(shard, k)], wfull.at[at(shard, k)], ags_sem, agr_sem.at[k], far)

    def forward(k):
        return remote(wfull.at[at(far_shard, k)], wfull.at[at(far_shard, k)], fws_sem, fwr_sem.at[k], pair)

    own_block = remote(
        wfull.at[at(shard, 0, rows)], wfull.at[at(shard, 0, rows)], own_sem.at[0], own_sem.at[1], pair
    )

    def partial_copy(k):
        return remote(part_out.at[k], part_in.at[k], ps_sem, pr_sem.at[k], far)

    def gossip(k):
        return remote(ubuf.at[k], nbuf.at[k], gs_sem, gr_sem.at[k], target)

    def to_relay(k, r):
        return remote(ubuf.at[k], rbuf.at[k], gs_sem, rr_sem.at[k], device(True, row + r))

    def from_relay(k, r):
        return remote(rbuf.at[k], nbuf.at[k], rf_sem.at[k], gr_sem.at[k], device(False, row - r + distance))

    def takes(k, r):
        return functools.reduce(jnp.logical_or, [k == i for i in range(CHUNKS) if routes[i] == r])

    def send_gossip(k):
        for r in relayed:
            pl.when(takes(k, r) & crossing)(lambda: to_relay(k, r).start())
        if distance in routes:
            pl.when(takes(k, distance) | jnp.logical_not(crossing))(lambda: gossip(k).start())
        else:
            pl.when(jnp.logical_not(crossing))(lambda: gossip(k).start())

    def relaying(k, act, offsets=relayed):
        for r in offsets:
            origin = lax.rem(row - r + 2 * block, block)
            pl.when(takes(k, r) & (origin + distance >= block))(lambda: act(k, r))

    def pass_on(k, r):
        to_relay(k, r).wait_recv()
        from_relay(k, r).start()

    gather(0).start()
    own_block.start()
    give[0].wait_recv()
    give[1].wait_recv()

    def grad_chunk(which, slot, k):
        columns = pl.ds(pl.multiple_of(k * chunk, chunk), chunk)
        mine = lax.dot_general(
            x_own[:, at(which, k)], dy_own[...], TOKENS_MAJOR, preferred_element_type=F32
        )
        return mine + lax.dot_general(
            x_pair[slot, :, columns], dy_pair[...], TOKENS_MAJOR, preferred_element_type=F32
        )

    def partials(k, carry):
        part_out[k] = grad_chunk(far_shard, 0, k).astype(BF16)

        @pl.when(k > 0)
        def _():
            partial_copy(k - 1).start()

        return carry

    lax.fori_loop(0, CHUNKS, partials, 0)
    kacc[...] = jnp.zeros_like(kacc)
    partial_copy(CHUNKS - 1).start()

    def project(which, k):
        block = wfull[at(which, k), :]
        kacc[...] += jnp.dot(x_own[:, at(which, k)], block, preferred_element_type=F32)
        dx_ref[:, at(which, k)] = lax.dot_general(
            dy_own[...], block, FEATURES_MINOR, preferred_element_type=F32
        ).astype(BF16)

    def part_of(k):
        return pl.ds(pl.multiple_of(k * chunk, chunk), chunk)

    loads[3].wait()
    loads[4].wait()
    give[2].wait_recv()
    own_block.wait_recv()
    count = jnp.full((8, 128), step_ref[0] + 1, jnp.int32).astype(F32)
    scale1 = (1.0 / (1.0 - jnp.exp(count * math.log(0.9))))[:1, :1]
    scale2 = (1.0 / (1.0 - jnp.exp(count * math.log(0.95))))[:1, :1]

    def start_gather(k, carry):
        gather(k).start()
        return carry

    def update(k, carry):
        mine = grad_chunk(shard, 1, k)
        at_once = jnp.logical_not(crossing) if relayed else k >= 0
        pl.when((k < CHUNKS - 1) & at_once)(lambda: gather(k + 1).start())

        partial_copy(k).wait_recv()
        grad = mine + part_in[k].astype(F32)
        part = part_of(k)
        first = 0.9 * m1buf[part, :].astype(F32) + 0.1 * grad
        second = 0.95 * m2buf[part, :].astype(F32) + 0.05 * grad * grad
        mom1_out[part, :] = first.astype(BF16)
        mom2_out[part, :] = second.astype(BF16)
        weight = wbuf[part, :]
        new = weight - 0.003 * ((first * scale1) / (jnp.sqrt(second * scale2) + 1e-08) + 0.1 * weight)
        wbuf[part, :] = new
        ubuf[k] = new.astype(BF16)
        project(shard, k)
        send_gossip(k)

        if relayed:
            @pl.when((k == CHUNKS - 1) & crossing)
            def _():
                lax.fori_loop(1, CHUNKS, start_gather, 0)

        project(pair_shard, k)

        @pl.when(k >= RELAY_LAG)
        def _():
            relaying(k - RELAY_LAG, pass_on, [r for r in relayed if r != 0])

        return carry

    lax.fori_loop(0, CHUNKS, update, 0)

    def finish(k, carry):
        @pl.when(k == 1)
        def _():
            def pass_rest(j, carry):
                relaying(j, pass_on, [r for r in relayed if r == 0])
                pl.when(j >= CHUNKS - RELAY_LAG)(lambda: relaying(j, pass_on, [r for r in relayed if r != 0]))
                return carry

            if relayed:
                lax.fori_loop(0, CHUNKS, pass_rest, 0)

        gather(k).wait_recv()
        forward(k).start()
        project(far_shard, k)
        forward(k).wait_recv()
        project(diag_shard, k)

        @pl.when(k > 1)
        def _():
            settle(k - 2)

        return carry

    def settle(k):
        gossip(k).wait_recv()
        part = part_of(k)
        wnext_ref[part, :] = 0.5 * (wbuf[part, :] + nbuf[k].astype(F32))

    lax.fori_loop(0, CHUNKS, finish, 0)
    keys_ref[...] = kacc[...].astype(BF16)

    def settle_rest(k, carry):
        settle(k)
        return carry

    lax.fori_loop(CHUNKS - 2, CHUNKS, settle_rest, 0)

    for copy in give:
        copy.wait_send()
    own_block.wait_send()

    remote(wfull.at[at(shard, 0, rows)], wfull.at[at(shard, 0, rows)], ags_sem, agr_sem.at[0], far).wait_send()
    remote(wfull.at[at(far_shard, 0, rows)], wfull.at[at(far_shard, 0, rows)], fws_sem, fwr_sem.at[0], pair).wait_send()
    remote(part_out, part_in, ps_sem, pr_sem.at[0], far).wait_send()
    remote(ubuf, nbuf, gs_sem, gr_sem.at[0], target).wait_send()

    def drain(k, carry):
        relaying(k, lambda k, r: from_relay(k, r).wait_send())
        return carry

    if relayed:
        lax.fori_loop(0, CHUNKS, drain, 0)


def make_train(level, replicas):
    distance = 2**level % replicas
    routes = ROUTES[level]

    def train(step, hidden, cotangent, weight, moment1, moment2):
        (tokens, width), (rows, features) = hidden.shape, weight.shape
        chunk = rows // CHUNKS
        dma = pltpu.SemaphoreType.DMA
        per_chunk = dma((CHUNKS,))
        hbm = pl.BlockSpec(memory_space=pl.ANY)
        outs = pl.pallas_call(
            functools.partial(train_kernel, distance, routes),
            name=f"train_{distance}",
            out_shape=(
                jax.ShapeDtypeStruct((tokens, features), BF16),
                jax.ShapeDtypeStruct((tokens, width), BF16),
                jax.ShapeDtypeStruct((rows, features), F32),
                jax.ShapeDtypeStruct((rows, features), BF16),
                jax.ShapeDtypeStruct((rows, features), BF16),
            ),
            in_specs=[pl.BlockSpec(memory_space=pltpu.SMEM)] + [hbm] * 5,
            out_specs=(pl.BlockSpec(memory_space=pltpu.VMEM),) * 5,
            scratch_shapes=[
                pltpu.VMEM((tokens, width), BF16),
                pltpu.VMEM((2, tokens, rows), BF16),
                pltpu.VMEM((tokens, features), BF16),
                pltpu.VMEM((tokens, features), BF16),
                pltpu.VMEM((rows, features), F32),
                pltpu.VMEM((rows, features), BF16),
                pltpu.VMEM((rows, features), BF16),
                pltpu.VMEM((width, features), BF16),
                pltpu.VMEM((CHUNKS, chunk, features), BF16),
                pltpu.VMEM((CHUNKS, chunk, features), BF16),
                pltpu.VMEM((CHUNKS, chunk, features), BF16),
                pltpu.VMEM((CHUNKS, chunk, features), BF16),
                pltpu.VMEM((CHUNKS, chunk, features), BF16),
                pltpu.VMEM((tokens, features), F32),
                dma((5,)),
                dma((3,)),
                dma((3,)),
                dma((2,)),
                dma,
                per_chunk,
                dma,
                per_chunk,
                dma,
                per_chunk,
                dma,
                per_chunk,
                per_chunk,
                per_chunk,
            ],
            compiler_params=pltpu.CompilerParams(
                collective_id=level, has_side_effects=True, vmem_limit_bytes=32 << 20
            ),
        )(step, hidden, cotangent, weight, moment1, moment2)
        return placed(outs)

    return train


PIECES = (1, 4, 4, 2, 2)


def placed_kernel(*refs):
    half = len(refs) // 2
    ins, outs, sem = refs[:half], refs[half:-1], refs[-1]
    copies = []
    for src, dst, pieces in zip(ins, outs, PIECES):
        size = src.shape[0] // pieces
        for i in range(pieces):
            part = pl.ds(i * size, size)
            copies.append(pltpu.make_async_copy(src.at[part], dst.at[part], sem.at[len(copies)]))
            copies[-1].start()
    for copy in copies:
        copy.wait()


def placed(values):
    hbm = pl.BlockSpec(memory_space=pl.ANY)
    return pl.pallas_call(
        placed_kernel,
        name="placed",
        out_shape=tuple(jax.ShapeDtypeStruct(v.shape, v.dtype) for v in values),
        in_specs=[hbm] * len(values),
        out_specs=(hbm,) * len(values),
        scratch_shapes=[pltpu.SemaphoreType.DMA((sum(PIECES),))],
        compiler_params=pltpu.CompilerParams(vmem_limit_bytes=1 << 20),
    )(*values)


def per_device(hidden, key_grad, weight, moment1, moment2, step):
    branches = [make_train(level, lax.axis_size("rep")) for level in range(LEVELS)]
    outs = lax.switch(
        step % LEVELS,
        branches,
        step.reshape(1),
        hidden[0],
        key_grad[0],
        weight[0],
        moment1[0],
        moment2[0],
    )
    return tuple(out[None] for out in outs)


def solution(mesh):
    blocks = P("rep", "fsdp", None)
    return jax.shard_map(
        per_device,
        mesh=mesh,
        in_specs=(blocks,) * 5 + (P(),),
        out_specs=(blocks,) * 5,
        check_vma=False,
    )
```

```python
import functools
import math

import jax
import jax.numpy as jnp
from jax import lax
from jax.experimental import pallas as pl
from jax.experimental.pallas import tpu as pltpu
from jax.sharding import PartitionSpec as P

LEVELS = 6
MESH = pl.DeviceIdType.MESH
F32 = jnp.float32
BF16 = jnp.bfloat16
CHUNKS = 8
NEAR = (-12, -16, -8, -4, -12, 0, 0)
ROUTES = ((1, *NEAR), (2, *NEAR), (-12, -8, -4, -16, -12, -8, 0, 0), (8, -12, 8, -12, -12, 0, 0, 0), (16, 16, 16, 0, 0, 0, 0, 0), (32,) * CHUNKS)
RELAY_LAG = 3
EAGER = 2
TOKENS_MAJOR = (((0,), (0,)), ((), ()))
FEATURES_MINOR = (((1,), (1,)), ((), ()))


def train_kernel(
    distance,
    routes,
    step_ref,
    hidden_ref,
    cot_ref,
    weight_ref,
    mom1_ref,
    mom2_ref,
    keys_ref,
    dx_ref,
    wnext_ref,
    mom1_out,
    mom2_out,
    x_own,
    x_pair,
    dy_own,
    dy_pair,
    wbuf,
    m1buf,
    m2buf,
    wfull,
    part_out,
    part_in,
    ubuf,
    nbuf,
    rbuf,
    kacc,
    load_sem,
    xs_sem,
    xr_sem,
    own_sem,
    ags_sem,
    agr_sem,
    fws_sem,
    fwr_sem,
    ps_sem,
    pr_sem,
    gs_sem,
    gr_sem,
    rr_sem,
    rf_sem,
):
    rep, shard = lax.axis_index("rep"), lax.axis_index("fsdp")
    replicas = lax.axis_size("rep")
    rows = weight_ref.shape[0]
    chunk = rows // CHUNKS
    core = lax.rem(shard, 2)
    half = shard // 2
    pair_shard = half * 2 + (1 - core)
    far_shard = (1 - half) * 2 + core
    diag_shard = (1 - half) * 2 + (1 - core)
    pair, far = (rep, pair_shard), (rep, far_shard)
    target = (lax.rem(rep + distance, replicas), shard)
    source = (lax.rem(rep - distance + replicas, replicas), shard)
    block = replicas // 2
    side, row = rep // block, lax.rem(rep, block)

    def device(other, r):
        return (1 - side if other else side) * block + lax.rem(r + 2 * block, block), shard

    crossing = row + distance >= block
    relayed = sorted(set(routes) - {distance})
    peers = [pair, far, target, source]
    for r in relayed:
        peers += [device(True, row + r), device(True, row - r)]
        peers += [device(False, row - r + distance), device(False, row + r - distance)]

    def at(which, k, size=chunk):
        return pl.ds(pl.multiple_of(which * rows + k * chunk, chunk), size)

    def remote(src, dst, send, recv, device):
        return pltpu.make_async_remote_copy(
            src_ref=src, dst_ref=dst, send_sem=send, recv_sem=recv, device_id=device, device_id_type=MESH
        )

    loads = [
        pltpu.make_async_copy(weight_ref, wbuf, load_sem.at[0]),
        pltpu.make_async_copy(cot_ref, dy_own, load_sem.at[1]),
        pltpu.make_async_copy(hidden_ref, x_own, load_sem.at[2]),
        pltpu.make_async_copy(mom1_ref, m1buf, load_sem.at[3]),
        pltpu.make_async_copy(mom2_ref, m2buf, load_sem.at[4]),
    ]
    for load in loads:
        load.start()

    barrier = pltpu.get_barrier_semaphore()
    for peer in peers:
        pl.semaphore_signal(barrier, inc=1, device_id=peer, device_id_type=MESH)
    loads[0].wait()

    def cast(k, carry):
        part = pl.ds(pl.multiple_of(k * chunk, chunk), chunk)
        wfull[at(shard, k), :] = wbuf[part, :].astype(BF16)
        return carry

    lax.fori_loop(0, CHUNKS, cast, 0)

    loads[1].wait()
    loads[2].wait()
    pl.semaphore_wait(barrier, len(peers))

    give = [
        remote(cot_ref, dy_pair, xs_sem.at[0], xr_sem.at[0], pair),
        remote(
            hidden_ref.at[:, at(diag_shard, 0, EAGER * chunk)],
            x_pair.at[0, :, pl.ds(0, EAGER * chunk)],
            xs_sem.at[1],
            xr_sem.at[1],
            pair,
        ),
        remote(
            hidden_ref.at[:, at(diag_shard, EAGER, rows - EAGER * chunk)],
            x_pair.at[0, :, pl.ds(EAGER * chunk, rows - EAGER * chunk)],
            xs_sem.at[2],
            xr_sem.at[2],
            pair,
        ),
        remote(hidden_ref.at[:, at(pair_shard, 0, rows)], x_pair.at[1], xs_sem.at[3], xr_sem.at[3], pair),
    ]
    for copy in give:
        copy.start()

    def gather(k):
        return remote(wfull.at[at(shard, k)], wfull.at[at(shard, k)], ags_sem, agr_sem.at[k], far)

    def forward(k):
        return remote(wfull.at[at(far_shard, k)], wfull.at[at(far_shard, k)], fws_sem, fwr_sem.at[k], pair)

    own_block = remote(
        wfull.at[at(shard, 0, rows)], wfull.at[at(shard, 0, rows)], own_sem.at[0], own_sem.at[1], pair
    )

    def partial_copy(k):
        return remote(part_out.at[k], part_in.at[k], ps_sem, pr_sem.at[k], far)

    def gossip(k):
        return remote(ubuf.at[k], nbuf.at[k], gs_sem, gr_sem.at[k], target)

    def to_relay(k, r):
        return remote(ubuf.at[k], rbuf.at[k], gs_sem, rr_sem.at[k], device(True, row + r))

    def from_relay(k, r):
        return remote(rbuf.at[k], nbuf.at[k], rf_sem.at[k], gr_sem.at[k], device(False, row - r + distance))

    def takes(k, r):
        return functools.reduce(jnp.logical_or, [k == i for i in range(CHUNKS) if routes[i] == r])

    def send_gossip(k):
        for r in relayed:
            pl.when(takes(k, r) & crossing)(lambda: to_relay(k, r).start())
        if distance in routes:
            pl.when(takes(k, distance) | jnp.logical_not(crossing))(lambda: gossip(k).start())
        else:
            pl.when(jnp.logical_not(crossing))(lambda: gossip(k).start())

    def relaying(k, act, offsets=relayed):
        for r in offsets:
            origin = lax.rem(row - r + 2 * block, block)
            pl.when(takes(k, r) & (origin + distance >= block))(lambda: act(k, r))

    def pass_on(k, r):
        to_relay(k, r).wait_recv()
        from_relay(k, r).start()

    gather(0).start()
    own_block.start()
    give[0].wait_recv()
    give[1].wait_recv()

    def grad_chunk(which, slot, k):
        columns = pl.ds(pl.multiple_of(k * chunk, chunk), chunk)
        mine = lax.dot_general(
            x_own[:, at(which, k)], dy_own[...], TOKENS_MAJOR, preferred_element_type=F32
        )
        return mine + lax.dot_general(
            x_pair[slot, :, columns], dy_pair[...], TOKENS_MAJOR, preferred_element_type=F32
        )

    def partials(k, carry):
        pl.when(k == EAGER)(lambda: give[2].wait_recv())
        part_out[k] = grad_chunk(far_shard, 0, k).astype(BF16)

        @pl.when(k > 0)
        def _():
            partial_copy(k - 1).start()

        return carry

    lax.fori_loop(0, CHUNKS, partials, 0)
    kacc[...] = jnp.zeros_like(kacc)
    partial_copy(CHUNKS - 1).start()

    def project(which, k):
        block = wfull[at(which, k), :]
        kacc[...] += jnp.dot(x_own[:, at(which, k)], block, preferred_element_type=F32)
        dx_ref[:, at(which, k)] = lax.dot_general(
            dy_own[...], block, FEATURES_MINOR, preferred_element_type=F32
        ).astype(BF16)

    def part_of(k):
        return pl.ds(pl.multiple_of(k * chunk, chunk), chunk)

    loads[3].wait()
    loads[4].wait()
    give[3].wait_recv()
    own_block.wait_recv()
    count = jnp.full((8, 128), step_ref[0] + 1, jnp.int32).astype(F32)
    scale1 = (1.0 / (1.0 - jnp.exp(count * math.log(0.9))))[:1, :1]
    scale2 = (1.0 / (1.0 - jnp.exp(count * math.log(0.95))))[:1, :1]

    def start_gather(k, carry):
        gather(k).start()
        return carry

    def update(k, carry):
        mine = grad_chunk(shard, 1, k)
        at_once = jnp.logical_not(crossing) if relayed else k >= 0
        pl.when((k < CHUNKS - 1) & at_once)(lambda: gather(k + 1).start())

        partial_copy(k).wait_recv()
        grad = mine + part_in[k].astype(F32)
        part = part_of(k)
        first = 0.9 * m1buf[part, :].astype(F32) + 0.1 * grad
        second = 0.95 * m2buf[part, :].astype(F32) + 0.05 * grad * grad
        mom1_out[part, :] = first.astype(BF16)
        mom2_out[part, :] = second.astype(BF16)
        weight = wbuf[part, :]
        new = weight - 0.003 * ((first * scale1) / (jnp.sqrt(second * scale2) + 1e-08) + 0.1 * weight)
        wbuf[part, :] = new
        ubuf[k] = new.astype(BF16)
        project(shard, k)
        send_gossip(k)

        if relayed:
            @pl.when((k == CHUNKS - 1) & crossing)
            def _():
                lax.fori_loop(1, CHUNKS, start_gather, 0)

        project(pair_shard, k)

        @pl.when(k >= RELAY_LAG)
        def _():
            relaying(k - RELAY_LAG, pass_on, [r for r in relayed if r != 0])

        return carry

    lax.fori_loop(0, CHUNKS, update, 0)

    def finish(k, carry):
        @pl.when(k == 0)
        def _():
            def pass_rest(j, carry):
                relaying(j, pass_on, [r for r in relayed if r == 0])
                pl.when(j >= CHUNKS - RELAY_LAG)(lambda: relaying(j, pass_on, [r for r in relayed if r != 0]))
                return carry

            if relayed:
                lax.fori_loop(0, CHUNKS, pass_rest, 0)

        gather(k).wait_recv()
        forward(k).start()
        project(far_shard, k)
        pl.when(k > 1)(lambda: settle(k - 2))
        pl.when(k == CHUNKS - 1)(lambda: settle(k - 1))
        forward(k).wait_recv()
        project(diag_shard, k)
        return carry

    def settle(k):
        gossip(k).wait_recv()
        part = part_of(k)
        wnext_ref[part, :] = 0.5 * (wbuf[part, :] + nbuf[k].astype(F32))

    lax.fori_loop(0, CHUNKS, finish, 0)
    keys_ref[...] = kacc[...].astype(BF16)

    settle(CHUNKS - 1)

    for copy in give:
        copy.wait_send()
    own_block.wait_send()

    remote(wfull.at[at(shard, 0, rows)], wfull.at[at(shard, 0, rows)], ags_sem, agr_sem.at[0], far).wait_send()
    remote(wfull.at[at(far_shard, 0, rows)], wfull.at[at(far_shard, 0, rows)], fws_sem, fwr_sem.at[0], pair).wait_send()
    remote(part_out, part_in, ps_sem, pr_sem.at[0], far).wait_send()
    remote(ubuf, nbuf, gs_sem, gr_sem.at[0], target).wait_send()

    def drain(k, carry):
        relaying(k, lambda k, r: from_relay(k, r).wait_send())
        return carry

    if relayed:
        lax.fori_loop(0, CHUNKS, drain, 0)


def make_train(level, replicas):
    distance = 2**level % replicas
    routes = ROUTES[level]

    def train(step, hidden, cotangent, weight, moment1, moment2):
        (tokens, width), (rows, features) = hidden.shape, weight.shape
        chunk = rows // CHUNKS
        dma = pltpu.SemaphoreType.DMA
        per_chunk = dma((CHUNKS,))
        hbm = pl.BlockSpec(memory_space=pl.ANY)
        outs = pl.pallas_call(
            functools.partial(train_kernel, distance, routes),
            name=f"train_{distance}",
            out_shape=(
                jax.ShapeDtypeStruct((tokens, features), BF16),
                jax.ShapeDtypeStruct((tokens, width), BF16),
                jax.ShapeDtypeStruct((rows, features), F32),
                jax.ShapeDtypeStruct((rows, features), BF16),
                jax.ShapeDtypeStruct((rows, features), BF16),
            ),
            in_specs=[pl.BlockSpec(memory_space=pltpu.SMEM)] + [hbm] * 5,
            out_specs=(pl.BlockSpec(memory_space=pltpu.VMEM),) * 5,
            scratch_shapes=[
                pltpu.VMEM((tokens, width), BF16),
                pltpu.VMEM((2, tokens, rows), BF16),
                pltpu.VMEM((tokens, features), BF16),
                pltpu.VMEM((tokens, features), BF16),
                pltpu.VMEM((rows, features), F32),
                pltpu.VMEM((rows, features), BF16),
                pltpu.VMEM((rows, features), BF16),
                pltpu.VMEM((width, features), BF16),
                pltpu.VMEM((CHUNKS, chunk, features), BF16),
                pltpu.VMEM((CHUNKS, chunk, features), BF16),
                pltpu.VMEM((CHUNKS, chunk, features), BF16),
                pltpu.VMEM((CHUNKS, chunk, features), BF16),
                pltpu.VMEM((CHUNKS, chunk, features), BF16),
                pltpu.VMEM((tokens, features), F32),
                dma((5,)),
                dma((4,)),
                dma((4,)),
                dma((2,)),
                dma,
                per_chunk,
                dma,
                per_chunk,
                dma,
                per_chunk,
                dma,
                per_chunk,
                per_chunk,
                per_chunk,
            ],
            compiler_params=pltpu.CompilerParams(
                collective_id=level, has_side_effects=True, vmem_limit_bytes=32 << 20
            ),
        )(step, hidden, cotangent, weight, moment1, moment2)
        return placed(outs)

    return train


PIECES = (1, 1, 1, 1, 1)


def placed_kernel(*refs):
    half = len(refs) // 2
    ins, outs, sem = refs[:half], refs[half:-1], refs[-1]
    copies = []
    for src, dst, pieces in zip(ins, outs, PIECES):
        size = src.shape[0] // pieces
        for i in range(pieces):
            part = pl.ds(i * size, size)
            copies.append(pltpu.make_async_copy(src.at[part], dst.at[part], sem.at[len(copies)]))
            copies[-1].start()
    for copy in copies:
        copy.wait()


def placed(values):
    hbm = pl.BlockSpec(memory_space=pl.ANY)
    return pl.pallas_call(
        placed_kernel,
        name="placed",
        out_shape=tuple(jax.ShapeDtypeStruct(v.shape, v.dtype) for v in values),
        in_specs=[hbm] * len(values),
        out_specs=(hbm,) * len(values),
        scratch_shapes=[pltpu.SemaphoreType.DMA((sum(PIECES),))],
        compiler_params=pltpu.CompilerParams(vmem_limit_bytes=1 << 20),
    )(*values)


def per_device(hidden, key_grad, weight, moment1, moment2, step):
    branches = [make_train(level, lax.axis_size("rep")) for level in range(LEVELS)]
    outs = lax.switch(
        step % LEVELS,
        branches,
        step.reshape(1),
        hidden[0],
        key_grad[0],
        weight[0],
        moment1[0],
        moment2[0],
    )
    return tuple(out[None] for out in outs)


def solution(mesh):
    blocks = P("rep", "fsdp", None)
    return jax.shard_map(
        per_device,
        mesh=mesh,
        in_specs=(blocks,) * 5 + (P(),),
        out_specs=(blocks,) * 5,
        check_vma=False,
    )
```

```python
import functools
import math

import jax
import jax.numpy as jnp
from jax import lax
from jax.experimental import pallas as pl
from jax.experimental.pallas import tpu as pltpu
from jax.sharding import PartitionSpec as P

LEVELS = 6
MESH = pl.DeviceIdType.MESH
F32 = jnp.float32
BF16 = jnp.bfloat16
CHUNKS = 8
ROUTES = tuple((-24, -20, -16, -12, -8, d, -4, 0) for d in (1, 2, 4)) + (
    (8, -12, 8, -12, 8, 0, 0, 0),
    (16, 16, 16, 0, 0, 0, 0, 0),
    (32,) * CHUNKS,
)
RELAY_LAG = 3
EAGER = 2
TOKENS_MAJOR = (((0,), (0,)), ((), ()))
FEATURES_MINOR = (((1,), (1,)), ((), ()))


def train_kernel(
    distance,
    routes,
    step_ref,
    hidden_ref,
    cot_ref,
    weight_ref,
    mom1_ref,
    mom2_ref,
    keys_ref,
    dx_ref,
    wnext_ref,
    mom1_out,
    mom2_out,
    x_own,
    x_pair,
    dy_own,
    dy_pair,
    wbuf,
    m1buf,
    m2buf,
    wfull,
    part_out,
    part_in,
    ubuf,
    nbuf,
    rbuf,
    kacc,
    load_sem,
    xs_sem,
    xr_sem,
    own_sem,
    ags_sem,
    agr_sem,
    fws_sem,
    fwr_sem,
    ps_sem,
    pr_sem,
    gs_sem,
    gr_sem,
    rr_sem,
    rf_sem,
):
    rep, shard = lax.axis_index("rep"), lax.axis_index("fsdp")
    replicas = lax.axis_size("rep")
    rows = weight_ref.shape[0]
    chunk = rows // CHUNKS
    core = lax.rem(shard, 2)
    half = shard // 2
    pair_shard = half * 2 + (1 - core)
    far_shard = (1 - half) * 2 + core
    diag_shard = (1 - half) * 2 + (1 - core)
    pair, far = (rep, pair_shard), (rep, far_shard)
    target = (lax.rem(rep + distance, replicas), shard)
    source = (lax.rem(rep - distance + replicas, replicas), shard)
    block = replicas // 2
    side, row = rep // block, lax.rem(rep, block)

    def device(other, r):
        return (1 - side if other else side) * block + lax.rem(r + 2 * block, block), shard

    crossing = row + distance >= block
    relayed = sorted(set(routes) - {distance})
    direct = distance in routes
    wanted = 2 + jnp.where(crossing, len(relayed) + int(direct), 1)
    greeted = [(None, pair), (None, far), (None if direct else row >= distance, source)]
    for r in relayed:
        serves = lax.rem(row - r + 2 * block, block) + distance >= block
        wanted += jnp.where(serves, 1, 0)
        greeted.append((serves, device(True, row - r)))
        greeted.append((row < distance, device(False, row + r - distance)))

    def at(which, k, size=chunk):
        return pl.ds(pl.multiple_of(which * rows + k * chunk, chunk), size)

    def remote(src, dst, send, recv, device):
        return pltpu.make_async_remote_copy(
            src_ref=src, dst_ref=dst, send_sem=send, recv_sem=recv, device_id=device, device_id_type=MESH
        )

    loads = [
        pltpu.make_async_copy(weight_ref, wbuf, load_sem.at[0]),
        pltpu.make_async_copy(cot_ref, dy_own, load_sem.at[1]),
        pltpu.make_async_copy(hidden_ref, x_own, load_sem.at[2]),
        pltpu.make_async_copy(mom1_ref, m1buf, load_sem.at[3]),
        pltpu.make_async_copy(mom2_ref, m2buf, load_sem.at[4]),
    ]
    for load in loads:
        load.start()

    barrier = pltpu.get_barrier_semaphore()
    for when, peer in greeted:
        greet = functools.partial(pl.semaphore_signal, barrier, inc=1, device_id=peer, device_id_type=MESH)
        greet() if when is None else pl.when(when)(greet)
    loads[0].wait()

    def cast(k, carry):
        part = pl.ds(pl.multiple_of(k * chunk, chunk), chunk)
        wfull[at(shard, k), :] = wbuf[part, :].astype(BF16)
        return carry

    lax.fori_loop(0, CHUNKS, cast, 0)

    loads[1].wait()
    loads[2].wait()
    pl.semaphore_wait(barrier, wanted)

    give = [
        remote(cot_ref, dy_pair, xs_sem.at[0], xr_sem.at[0], pair),
        remote(
            hidden_ref.at[:, at(diag_shard, 0, EAGER * chunk)],
            x_pair.at[0, :, pl.ds(0, EAGER * chunk)],
            xs_sem.at[1],
            xr_sem.at[1],
            pair,
        ),
        remote(
            hidden_ref.at[:, at(diag_shard, EAGER, rows - EAGER * chunk)],
            x_pair.at[0, :, pl.ds(EAGER * chunk, rows - EAGER * chunk)],
            xs_sem.at[2],
            xr_sem.at[2],
            pair,
        ),
        remote(hidden_ref.at[:, at(pair_shard, 0, rows)], x_pair.at[1], xs_sem.at[3], xr_sem.at[3], pair),
    ]
    for copy in give:
        copy.start()

    def gather(k):
        return remote(wfull.at[at(shard, k)], wfull.at[at(shard, k)], ags_sem, agr_sem.at[k], far)

    def forward(k):
        return remote(wfull.at[at(far_shard, k)], wfull.at[at(far_shard, k)], fws_sem, fwr_sem.at[k], pair)

    own_block = remote(
        wfull.at[at(shard, 0, rows)], wfull.at[at(shard, 0, rows)], own_sem.at[0], own_sem.at[1], pair
    )

    def partial_copy(k):
        return remote(part_out.at[k], part_in.at[k], ps_sem, pr_sem.at[k], far)

    def gossip(k):
        return remote(ubuf.at[k], nbuf.at[k], gs_sem, gr_sem.at[k], target)

    def to_relay(k, r):
        return remote(ubuf.at[k], rbuf.at[k], gs_sem, rr_sem.at[k], device(True, row + r))

    def from_relay(k, r):
        return remote(rbuf.at[k], nbuf.at[k], rf_sem.at[k], gr_sem.at[k], device(False, row - r + distance))

    def takes(k, r):
        return functools.reduce(jnp.logical_or, [k == i for i in range(CHUNKS) if routes[i] == r])

    def send_gossip(k):
        for r in relayed:
            pl.when(takes(k, r) & crossing)(lambda: to_relay(k, r).start())
        if distance in routes:
            pl.when(takes(k, distance) | jnp.logical_not(crossing))(lambda: gossip(k).start())
        else:
            pl.when(jnp.logical_not(crossing))(lambda: gossip(k).start())

    def relaying(k, act, offsets=relayed):
        for r in offsets:
            origin = lax.rem(row - r + 2 * block, block)
            pl.when(takes(k, r) & (origin + distance >= block))(lambda: act(k, r))

    def pass_on(k, r):
        to_relay(k, r).wait_recv()
        from_relay(k, r).start()

    gather(0).start()
    own_block.start()
    give[0].wait_recv()
    give[1].wait_recv()

    def grad_chunk(which, slot, k):
        columns = pl.ds(pl.multiple_of(k * chunk, chunk), chunk)
        mine = lax.dot_general(
            x_own[:, at(which, k)], dy_own[...], TOKENS_MAJOR, preferred_element_type=F32
        )
        return mine + lax.dot_general(
            x_pair[slot, :, columns], dy_pair[...], TOKENS_MAJOR, preferred_element_type=F32
        )

    def partials(k, carry):
        pl.when(k == EAGER)(lambda: give[2].wait_recv())
        part_out[k] = grad_chunk(far_shard, 0, k).astype(BF16)

        @pl.when(k > 0)
        def _():
            partial_copy(k - 1).start()

        return carry

    lax.fori_loop(0, CHUNKS, partials, 0)
    kacc[...] = jnp.zeros_like(kacc)
    partial_copy(CHUNKS - 1).start()

    def project(which, k):
        block = wfull[at(which, k), :]
        kacc[...] += jnp.dot(x_own[:, at(which, k)], block, preferred_element_type=F32)
        dx_ref[:, at(which, k)] = lax.dot_general(
            dy_own[...], block, FEATURES_MINOR, preferred_element_type=F32
        ).astype(BF16)

    def part_of(k):
        return pl.ds(pl.multiple_of(k * chunk, chunk), chunk)

    loads[3].wait()
    loads[4].wait()
    give[3].wait_recv()
    own_block.wait_recv()
    count = jnp.full((8, 128), step_ref[0] + 1, jnp.int32).astype(F32)
    scale1 = (1.0 / (1.0 - jnp.exp(count * math.log(0.9))))[:1, :1]
    scale2 = (1.0 / (1.0 - jnp.exp(count * math.log(0.95))))[:1, :1]

    def start_gather(k, carry):
        gather(k).start()
        return carry

    def update(k, carry):
        mine = grad_chunk(shard, 1, k)
        at_once = jnp.logical_not(crossing) if relayed else k >= 0
        pl.when((k < CHUNKS - 1) & at_once)(lambda: gather(k + 1).start())

        partial_copy(k).wait_recv()
        grad = mine + part_in[k].astype(F32)
        part = part_of(k)
        first = 0.9 * m1buf[part, :].astype(F32) + 0.1 * grad
        second = 0.95 * m2buf[part, :].astype(F32) + 0.05 * grad * grad
        mom1_out[part, :] = first.astype(BF16)
        mom2_out[part, :] = second.astype(BF16)
        weight = wbuf[part, :]
        new = weight - 0.003 * ((first * scale1) / (jnp.sqrt(second * scale2) + 1e-08) + 0.1 * weight)
        wbuf[part, :] = new
        ubuf[k] = new.astype(BF16)
        project(shard, k)
        send_gossip(k)

        if relayed:
            ahead = 1 if 0 in routes[: CHUNKS - 1] else 3
            if ahead > 1:

                @pl.when((k == CHUNKS - 2) & crossing)
                def _():
                    lax.fori_loop(1, ahead, start_gather, 0)

            @pl.when((k == CHUNKS - 1) & crossing)
            def _():
                lax.fori_loop(ahead, CHUNKS, start_gather, 0)

        project(pair_shard, k)

        @pl.when(k >= RELAY_LAG)
        def _():
            relaying(k - RELAY_LAG, pass_on, [r for r in relayed if r != 0])

        return carry

    lax.fori_loop(0, CHUNKS, update, 0)

    def finish(k, carry):
        @pl.when(k == 0)
        def _():
            def pass_rest(j, carry):
                relaying(j, pass_on, [r for r in relayed if r == 0])
                pl.when(j >= CHUNKS - RELAY_LAG)(lambda: relaying(j, pass_on, [r for r in relayed if r != 0]))
                return carry

            if relayed:
                lax.fori_loop(0, CHUNKS, pass_rest, 0)

        gather(k).wait_recv()
        forward(k).start()
        project(far_shard, k)
        pl.when(k > 1)(lambda: settle(k - 2))
        pl.when(k == CHUNKS - 1)(lambda: settle(k - 1))
        forward(k).wait_recv()
        project(diag_shard, k)
        return carry

    def settle(k):
        gossip(k).wait_recv()
        part = part_of(k)
        wnext_ref[part, :] = 0.5 * (wbuf[part, :] + nbuf[k].astype(F32))

    lax.fori_loop(0, CHUNKS, finish, 0)
    keys_ref[...] = kacc[...].astype(BF16)

    settle(CHUNKS - 1)

    for copy in give:
        copy.wait_send()
    own_block.wait_send()

    remote(wfull.at[at(shard, 0, rows)], wfull.at[at(shard, 0, rows)], ags_sem, agr_sem.at[0], far).wait_send()
    remote(wfull.at[at(far_shard, 0, rows)], wfull.at[at(far_shard, 0, rows)], fws_sem, fwr_sem.at[0], pair).wait_send()
    remote(part_out, part_in, ps_sem, pr_sem.at[0], far).wait_send()
    remote(ubuf, nbuf, gs_sem, gr_sem.at[0], target).wait_send()

    def drain(k, carry):
        relaying(k, lambda k, r: from_relay(k, r).wait_send())
        return carry

    if relayed:
        lax.fori_loop(0, CHUNKS, drain, 0)


def make_train(level, replicas):
    distance = 2**level % replicas
    routes = ROUTES[level]

    def train(step, hidden, cotangent, weight, moment1, moment2):
        (tokens, width), (rows, features) = hidden.shape, weight.shape
        chunk = rows // CHUNKS
        dma = pltpu.SemaphoreType.DMA
        per_chunk = dma((CHUNKS,))
        hbm = pl.BlockSpec(memory_space=pl.ANY)
        outs = pl.pallas_call(
            functools.partial(train_kernel, distance, routes),
            name=f"train_{distance}",
            out_shape=(
                jax.ShapeDtypeStruct((tokens, features), BF16),
                jax.ShapeDtypeStruct((tokens, width), BF16),
                jax.ShapeDtypeStruct((rows, features), F32),
                jax.ShapeDtypeStruct((rows, features), BF16),
                jax.ShapeDtypeStruct((rows, features), BF16),
            ),
            in_specs=[pl.BlockSpec(memory_space=pltpu.SMEM)] + [hbm] * 5,
            out_specs=(pl.BlockSpec(memory_space=pltpu.VMEM),) * 5,
            scratch_shapes=[
                pltpu.VMEM((tokens, width), BF16),
                pltpu.VMEM((2, tokens, rows), BF16),
                pltpu.VMEM((tokens, features), BF16),
                pltpu.VMEM((tokens, features), BF16),
                pltpu.VMEM((rows, features), F32),
                pltpu.VMEM((rows, features), BF16),
                pltpu.VMEM((rows, features), BF16),
                pltpu.VMEM((width, features), BF16),
                pltpu.VMEM((CHUNKS, chunk, features), BF16),
                pltpu.VMEM((CHUNKS, chunk, features), BF16),
                pltpu.VMEM((CHUNKS, chunk, features), BF16),
                pltpu.VMEM((CHUNKS, chunk, features), BF16),
                pltpu.VMEM((CHUNKS, chunk, features), BF16),
                pltpu.VMEM((tokens, features), F32),
                dma((5,)),
                dma((4,)),
                dma((4,)),
                dma((2,)),
                dma,
                per_chunk,
                dma,
                per_chunk,
                dma,
                per_chunk,
                dma,
                per_chunk,
                per_chunk,
                per_chunk,
            ],
            compiler_params=pltpu.CompilerParams(
                collective_id=level, has_side_effects=True, vmem_limit_bytes=32 << 20
            ),
        )(step, hidden, cotangent, weight, moment1, moment2)
        return placed(outs)

    return train


PIECES = (1, 1, 1, 1, 1)


def placed_kernel(*refs):
    half = len(refs) // 2
    ins, outs, sem = refs[:half], refs[half:-1], refs[-1]
    copies = []
    for src, dst, pieces in zip(ins, outs, PIECES):
        size = src.shape[0] // pieces
        for i in range(pieces):
            part = pl.ds(i * size, size)
            copies.append(pltpu.make_async_copy(src.at[part], dst.at[part], sem.at[len(copies)]))
            copies[-1].start()
    for copy in copies:
        copy.wait()


def placed(values):
    hbm = pl.BlockSpec(memory_space=pl.ANY)
    return pl.pallas_call(
        placed_kernel,
        name="placed",
        out_shape=tuple(jax.ShapeDtypeStruct(v.shape, v.dtype) for v in values),
        in_specs=[hbm] * len(values),
        out_specs=(hbm,) * len(values),
        scratch_shapes=[pltpu.SemaphoreType.DMA((sum(PIECES),))],
        compiler_params=pltpu.CompilerParams(vmem_limit_bytes=1 << 20),
    )(*values)


def per_device(hidden, key_grad, weight, moment1, moment2, step):
    branches = [make_train(level, lax.axis_size("rep")) for level in range(LEVELS)]
    outs = lax.switch(
        step % LEVELS,
        branches,
        step.reshape(1),
        hidden[0],
        key_grad[0],
        weight[0],
        moment1[0],
        moment2[0],
    )
    return tuple(out[None] for out in outs)


def solution(mesh):
    blocks = P("rep", "fsdp", None)
    return jax.shard_map(
        per_device,
        mesh=mesh,
        in_specs=(blocks,) * 5 + (P(),),
        out_specs=(blocks,) * 5,
        check_vma=False,
    )
```

```python
import functools
import math

import jax
import jax.numpy as jnp
from jax import lax
from jax.experimental import pallas as pl
from jax.experimental.pallas import tpu as pltpu
from jax.sharding import PartitionSpec as P

LEVELS = 6
MESH = pl.DeviceIdType.MESH
F32 = jnp.float32
BF16 = jnp.bfloat16
CHUNKS = 8
ROUTES = tuple((-24, -20, -16, -12, -8, d, -4, 0) for d in (1, 2, 4)) + (
    (8, -12, 8, -12, 8, 0, 0, 0),
    (16, 16, 16, 0, 0, 0, 0, 0),
    (32,) * CHUNKS,
)
RELAY_LAG = 3
EAGER = 2
TOKENS_MAJOR = (((0,), (0,)), ((), ()))
FEATURES_MINOR = (((1,), (1,)), ((), ()))


def train_kernel(
    distance,
    routes,
    step_ref,
    hidden_ref,
    cot_ref,
    weight_ref,
    mom1_ref,
    mom2_ref,
    keys_ref,
    dx_ref,
    wnext_ref,
    mom1_out,
    mom2_out,
    x_own,
    x_pair,
    dy_own,
    dy_pair,
    wbuf,
    m1buf,
    m2buf,
    wfull,
    part_out,
    part_in,
    ubuf,
    nbuf,
    rbuf,
    kacc,
    load_sem,
    xs_sem,
    xr_sem,
    own_sem,
    ags_sem,
    agr_sem,
    fws_sem,
    fwr_sem,
    ps_sem,
    pr_sem,
    gs_sem,
    gr_sem,
    rr_sem,
    rf_sem,
):
    rep, shard = lax.axis_index("rep"), lax.axis_index("fsdp")
    replicas = lax.axis_size("rep")
    rows = weight_ref.shape[0]
    chunk = rows // CHUNKS
    core = lax.rem(shard, 2)
    half = shard // 2
    pair_shard = half * 2 + (1 - core)
    far_shard = (1 - half) * 2 + core
    diag_shard = (1 - half) * 2 + (1 - core)
    pair, far = (rep, pair_shard), (rep, far_shard)
    target = (lax.rem(rep + distance, replicas), shard)
    source = (lax.rem(rep - distance + replicas, replicas), shard)
    block = replicas // 2
    side, row = rep // block, lax.rem(rep, block)

    def device(other, r):
        return (1 - side if other else side) * block + lax.rem(r + 2 * block, block), shard

    crossing = row + distance >= block
    relayed = sorted(set(routes) - {distance})
    direct = distance in routes
    wanted = 2 + jnp.where(crossing, len(relayed) + int(direct), 1)
    greeted = [(None, pair), (None, far), (None if direct else row >= distance, source)]
    for r in relayed:
        serves = lax.rem(row - r + 2 * block, block) + distance >= block
        wanted += jnp.where(serves, 1, 0)
        greeted.append((serves, device(True, row - r)))
        greeted.append((row < distance, device(False, row + r - distance)))

    def at(which, k, size=chunk):
        return pl.ds(pl.multiple_of(which * rows + k * chunk, chunk), size)

    def remote(src, dst, send, recv, device):
        return pltpu.make_async_remote_copy(
            src_ref=src, dst_ref=dst, send_sem=send, recv_sem=recv, device_id=device, device_id_type=MESH
        )

    loads = [
        pltpu.make_async_copy(weight_ref.at[pl.ds(0, chunk)], wbuf.at[pl.ds(0, chunk)], load_sem.at[0]),
        pltpu.make_async_copy(cot_ref, dy_own, load_sem.at[1]),
        pltpu.make_async_copy(hidden_ref, x_own, load_sem.at[2]),
        pltpu.make_async_copy(mom1_ref, m1buf, load_sem.at[3]),
        pltpu.make_async_copy(mom2_ref, m2buf, load_sem.at[4]),
        pltpu.make_async_copy(
            weight_ref.at[pl.ds(chunk, rows - chunk)], wbuf.at[pl.ds(chunk, rows - chunk)], load_sem.at[5]
        ),
    ]
    for i in (0, 1, 2, 5, 3, 4):
        loads[i].start()

    barrier = pltpu.get_barrier_semaphore()
    for when, peer in greeted:
        greet = functools.partial(pl.semaphore_signal, barrier, inc=1, device_id=peer, device_id_type=MESH)
        greet() if when is None else pl.when(when)(greet)
    loads[0].wait()

    def cast(k, carry):
        part = pl.ds(pl.multiple_of(k * chunk, chunk), chunk)
        wfull[at(shard, k), :] = wbuf[part, :].astype(BF16)
        return carry

    cast(0, 0)
    pl.semaphore_wait(barrier, wanted)

    give = [
        remote(cot_ref, dy_pair, xs_sem.at[0], xr_sem.at[0], pair),
        remote(
            hidden_ref.at[:, at(diag_shard, 0, EAGER * chunk)],
            x_pair.at[0, :, pl.ds(0, EAGER * chunk)],
            xs_sem.at[1],
            xr_sem.at[1],
            pair,
        ),
        remote(
            hidden_ref.at[:, at(diag_shard, EAGER, rows - EAGER * chunk)],
            x_pair.at[0, :, pl.ds(EAGER * chunk, rows - EAGER * chunk)],
            xs_sem.at[2],
            xr_sem.at[2],
            pair,
        ),
        remote(hidden_ref.at[:, at(pair_shard, 0, rows)], x_pair.at[1], xs_sem.at[3], xr_sem.at[3], pair),
    ]
    for copy in give:
        copy.start()

    def gather(k):
        return remote(wfull.at[at(shard, k)], wfull.at[at(shard, k)], ags_sem, agr_sem.at[k], far)

    def forward(k):
        return remote(wfull.at[at(far_shard, k)], wfull.at[at(far_shard, k)], fws_sem, fwr_sem.at[k], pair)

    own_block = remote(
        wfull.at[at(shard, 0, rows)], wfull.at[at(shard, 0, rows)], own_sem.at[0], own_sem.at[1], pair
    )

    def partial_copy(k):
        return remote(part_out.at[k], part_in.at[k], ps_sem, pr_sem.at[k], far)

    def gossip(k):
        return remote(ubuf.at[k], nbuf.at[k], gs_sem, gr_sem.at[k], target)

    def to_relay(k, r):
        return remote(ubuf.at[k], rbuf.at[k], gs_sem, rr_sem.at[k], device(True, row + r))

    def from_relay(k, r):
        return remote(rbuf.at[k], nbuf.at[k], rf_sem.at[k], gr_sem.at[k], device(False, row - r + distance))

    def takes(k, r):
        return functools.reduce(jnp.logical_or, [k == i for i in range(CHUNKS) if routes[i] == r])

    def send_gossip(k):
        for r in relayed:
            pl.when(takes(k, r) & crossing)(lambda: to_relay(k, r).start())
        if distance in routes:
            pl.when(takes(k, distance) | jnp.logical_not(crossing))(lambda: gossip(k).start())
        else:
            pl.when(jnp.logical_not(crossing))(lambda: gossip(k).start())

    def relaying(k, act, offsets=relayed):
        for r in offsets:
            origin = lax.rem(row - r + 2 * block, block)
            pl.when(takes(k, r) & (origin + distance >= block))(lambda: act(k, r))

    def pass_on(k, r):
        to_relay(k, r).wait_recv()
        from_relay(k, r).start()

    gather(0).start()
    loads[5].wait()
    lax.fori_loop(1, CHUNKS, cast, 0)
    own_block.start()
    loads[1].wait()
    loads[2].wait()
    give[0].wait_recv()
    give[1].wait_recv()

    def grad_chunk(which, slot, k):
        columns = pl.ds(pl.multiple_of(k * chunk, chunk), chunk)
        mine = lax.dot_general(
            x_own[:, at(which, k)], dy_own[...], TOKENS_MAJOR, preferred_element_type=F32
        )
        return mine + lax.dot_general(
            x_pair[slot, :, columns], dy_pair[...], TOKENS_MAJOR, preferred_element_type=F32
        )

    def partials(k, carry):
        pl.when(k == EAGER)(lambda: give[2].wait_recv())
        part_out[k] = grad_chunk(far_shard, 0, k).astype(BF16)

        @pl.when(k > 0)
        def _():
            partial_copy(k - 1).start()

        return carry

    lax.fori_loop(0, CHUNKS, partials, 0)
    kacc[...] = jnp.zeros_like(kacc)
    partial_copy(CHUNKS - 1).start()

    def project(which, k):
        block = wfull[at(which, k), :]
        kacc[...] += jnp.dot(x_own[:, at(which, k)], block, preferred_element_type=F32)
        dx_ref[:, at(which, k)] = lax.dot_general(
            dy_own[...], block, FEATURES_MINOR, preferred_element_type=F32
        ).astype(BF16)

    def part_of(k):
        return pl.ds(pl.multiple_of(k * chunk, chunk), chunk)

    loads[3].wait()
    loads[4].wait()
    give[3].wait_recv()
    own_block.wait_recv()
    count = jnp.full((8, 128), step_ref[0] + 1, jnp.int32).astype(F32)
    scale1 = (1.0 / (1.0 - jnp.exp(count * math.log(0.9))))[:1, :1]
    scale2 = (1.0 / (1.0 - jnp.exp(count * math.log(0.95))))[:1, :1]

    def start_gather(k, carry):
        gather(k).start()
        return carry

    def update(k, carry):
        mine = grad_chunk(shard, 1, k)
        at_once = jnp.logical_not(crossing) if relayed else k >= 0
        pl.when((k < CHUNKS - 1) & at_once)(lambda: gather(k + 1).start())

        partial_copy(k).wait_recv()
        grad = mine + part_in[k].astype(F32)
        part = part_of(k)
        first = 0.9 * m1buf[part, :].astype(F32) + 0.1 * grad
        second = 0.95 * m2buf[part, :].astype(F32) + 0.05 * grad * grad
        mom1_out[part, :] = first.astype(BF16)
        mom2_out[part, :] = second.astype(BF16)
        weight = wbuf[part, :]
        new = weight - 0.003 * ((first * scale1) / (jnp.sqrt(second * scale2) + 1e-08) + 0.1 * weight)
        wbuf[part, :] = new
        ubuf[k] = new.astype(BF16)
        project(shard, k)
        send_gossip(k)

        if relayed:
            ahead = 1 if 0 in routes[: CHUNKS - 1] else 3
            if ahead > 1:

                @pl.when((k == CHUNKS - 2) & crossing)
                def _():
                    lax.fori_loop(1, ahead, start_gather, 0)

            @pl.when((k == CHUNKS - 1) & crossing)
            def _():
                lax.fori_loop(ahead, CHUNKS, start_gather, 0)

        project(pair_shard, k)

        @pl.when(k >= RELAY_LAG)
        def _():
            relaying(k - RELAY_LAG, pass_on, [r for r in relayed if r != 0])

        return carry

    lax.fori_loop(0, CHUNKS, update, 0)

    def finish(k, carry):
        @pl.when(k == 0)
        def _():
            def pass_rest(j, carry):
                relaying(j, pass_on, [r for r in relayed if r == 0])
                pl.when(j >= CHUNKS - RELAY_LAG)(lambda: relaying(j, pass_on, [r for r in relayed if r != 0]))
                return carry

            if relayed:
                lax.fori_loop(0, CHUNKS, pass_rest, 0)

        gather(k).wait_recv()
        forward(k).start()
        project(far_shard, k)
        pl.when(k > 1)(lambda: settle(k - 2))
        pl.when(k == CHUNKS - 1)(lambda: settle(k - 1))
        forward(k).wait_recv()
        project(diag_shard, k)
        return carry

    def settle(k):
        gossip(k).wait_recv()
        part = part_of(k)
        wnext_ref[part, :] = 0.5 * (wbuf[part, :] + nbuf[k].astype(F32))

    lax.fori_loop(0, CHUNKS, finish, 0)
    keys_ref[...] = kacc[...].astype(BF16)

    settle(CHUNKS - 1)

    for copy in give:
        copy.wait_send()
    own_block.wait_send()

    remote(wfull.at[at(shard, 0, rows)], wfull.at[at(shard, 0, rows)], ags_sem, agr_sem.at[0], far).wait_send()
    remote(wfull.at[at(far_shard, 0, rows)], wfull.at[at(far_shard, 0, rows)], fws_sem, fwr_sem.at[0], pair).wait_send()
    remote(part_out, part_in, ps_sem, pr_sem.at[0], far).wait_send()
    remote(ubuf, nbuf, gs_sem, gr_sem.at[0], target).wait_send()

    def drain(k, carry):
        relaying(k, lambda k, r: from_relay(k, r).wait_send())
        return carry

    if relayed:
        lax.fori_loop(0, CHUNKS, drain, 0)


def make_train(level, replicas):
    distance = 2**level % replicas
    routes = ROUTES[level]

    def train(step, hidden, cotangent, weight, moment1, moment2):
        (tokens, width), (rows, features) = hidden.shape, weight.shape
        chunk = rows // CHUNKS
        dma = pltpu.SemaphoreType.DMA
        per_chunk = dma((CHUNKS,))
        hbm = pl.BlockSpec(memory_space=pl.ANY)
        outs = pl.pallas_call(
            functools.partial(train_kernel, distance, routes),
            name=f"train_{distance}",
            out_shape=(
                jax.ShapeDtypeStruct((tokens, features), BF16),
                jax.ShapeDtypeStruct((tokens, width), BF16),
                jax.ShapeDtypeStruct((rows, features), F32),
                jax.ShapeDtypeStruct((rows, features), BF16),
                jax.ShapeDtypeStruct((rows, features), BF16),
            ),
            in_specs=[pl.BlockSpec(memory_space=pltpu.SMEM)] + [hbm] * 5,
            out_specs=(pl.BlockSpec(memory_space=pltpu.VMEM),) * 5,
            scratch_shapes=[
                pltpu.VMEM((tokens, width), BF16),
                pltpu.VMEM((2, tokens, rows), BF16),
                pltpu.VMEM((tokens, features), BF16),
                pltpu.VMEM((tokens, features), BF16),
                pltpu.VMEM((rows, features), F32),
                pltpu.VMEM((rows, features), BF16),
                pltpu.VMEM((rows, features), BF16),
                pltpu.VMEM((width, features), BF16),
                pltpu.VMEM((CHUNKS, chunk, features), BF16),
                pltpu.VMEM((CHUNKS, chunk, features), BF16),
                pltpu.VMEM((CHUNKS, chunk, features), BF16),
                pltpu.VMEM((CHUNKS, chunk, features), BF16),
                pltpu.VMEM((CHUNKS, chunk, features), BF16),
                pltpu.VMEM((tokens, features), F32),
                dma((6,)),
                dma((4,)),
                dma((4,)),
                dma((2,)),
                dma,
                per_chunk,
                dma,
                per_chunk,
                dma,
                per_chunk,
                dma,
                per_chunk,
                per_chunk,
                per_chunk,
            ],
            compiler_params=pltpu.CompilerParams(
                collective_id=level, has_side_effects=True, vmem_limit_bytes=32 << 20
            ),
        )(step, hidden, cotangent, weight, moment1, moment2)
        return placed(outs)

    return train


PIECES = (1, 1, 1, 1, 1)


def placed_kernel(*refs):
    half = len(refs) // 2
    ins, outs, sem = refs[:half], refs[half:-1], refs[-1]
    copies = []
    for src, dst, pieces in zip(ins, outs, PIECES):
        size = src.shape[0] // pieces
        for i in range(pieces):
            part = pl.ds(i * size, size)
            copies.append(pltpu.make_async_copy(src.at[part], dst.at[part], sem.at[len(copies)]))
            copies[-1].start()
    for copy in copies:
        copy.wait()


def placed(values):
    hbm = pl.BlockSpec(memory_space=pl.ANY)
    return pl.pallas_call(
        placed_kernel,
        name="placed",
        out_shape=tuple(jax.ShapeDtypeStruct(v.shape, v.dtype) for v in values),
        in_specs=[hbm] * len(values),
        out_specs=(hbm,) * len(values),
        scratch_shapes=[pltpu.SemaphoreType.DMA((sum(PIECES),))],
        compiler_params=pltpu.CompilerParams(vmem_limit_bytes=1 << 20),
    )(*values)


def per_device(hidden, key_grad, weight, moment1, moment2, step):
    branches = [make_train(level, lax.axis_size("rep")) for level in range(LEVELS)]
    outs = lax.switch(
        lax.rem(step, LEVELS),
        branches,
        step.reshape(1),
        hidden[0],
        key_grad[0],
        weight[0],
        moment1[0],
        moment2[0],
    )
    return tuple(out[None] for out in outs)


def solution(mesh):
    blocks = P("rep", "fsdp", None)
    return jax.shard_map(
        per_device,
        mesh=mesh,
        in_specs=(blocks,) * 5 + (P(),),
        out_specs=(blocks,) * 5,
        check_vma=False,
    )
```
